32 devices in a mesh: groups: 1, seq: 16 (over z, y, x), section: 1, head: 2 (over core).
Axes of the slice: x: 2, y: 2, z: 4, core: 2. Of those that a mesh axis runs over, the one named last changes fastest.
Arguments:
- queries: bfloat16 [2560, 3072], P(('groups', 'seq', 'head'), 'section'), may hold values from -24 to 24
- keys: bfloat16 [2560, 3072], P(('groups', 'seq', 'head'), 'section'), may hold values from -10.5 to 10.5
- values: bfloat16 [2560, 3072], P(('groups', 'seq', 'head'), 'section'), may hold values from -6 to 6
- text_keys: bfloat16 [128, 3072], P(('groups', 'seq', 'head'), 'section'), may hold values from -10 to 10
- text_values: bfloat16 [128, 3072], P(('groups', 'seq', 'head'), 'section'), may hold values from -6 to 6
- text_length: int32 [1], P('groups'), may hold values from 32 to 128
- out_weight: bfloat16 [3072, 3072], P(None, 'section'), may hold values from -0.109375 to 0.109375
Outputs:
- projected: bfloat16 [2560, 3072], P(('groups', 'seq', 'head'), 'section')
The draws below stay inside these ranges and needn't reach their ends.
All inputs are finite; a program needn't handle non-finite values.
Results may differ from the reference program's by a relative error of at most 0.0065.
Values may be sent and summed in bfloat16 or wider, within the bound.
A program may use at most 128 MiB of HBM per device.

```python
import jax
import jax.numpy as jnp
from jax import lax

HEADS = 24
HEAD_DIM = 128
D = 3072
TXT = 128
TOKENS = 2560


spread = 1.7


def paired_draw(key):
    base = jax.random.fold_in(key, 41)
    query_key, keys_key = jax.random.split(base)
    query_draw = spread * jax.random.truncated_normal(query_key, -6.0, 6.0, (TOKENS, D), jnp.float32)
    keys_draw = spread * jax.random.truncated_normal(keys_key, -6.0, 6.0, (TOKENS, D), jnp.float32)
    return (query_draw, keys_draw)


def draw_queries(key, part):
    return paired_draw(key)[0].astype(jnp.bfloat16)


def draw_keys(key, part):
    return paired_draw(key)[1].astype(jnp.bfloat16)


def level_of(own_key, dims, pieces, least, high):
    def one(dim, blocks):
        steps = jax.random.uniform(jax.random.fold_in(jax.random.fold_in(own_key, 6), dim), (blocks,), jnp.float32, least / len(pieces), high / len(pieces))
        return jnp.repeat(jnp.exp(steps), dims[dim] // blocks).reshape((-1,) + (1,) * (len(dims) - dim - 1))

    factor_of = one(*pieces[0])
    for cut in pieces[1:]:
        factor_of = factor_of * one(*cut)
    return factor_of


def scatter_about(stream_key, dims, scale, limit, cuts=(), kind=jnp.bfloat16):
    array = jax.random.normal(stream_key, dims, jnp.float32) * scale
    if len(cuts) > 0:
        array = level_of(stream_key, dims, cuts, -0.22, 0.18) * array
    return jnp.clip(array, min=-limit, max=limit).astype(kind)


def setup_inputs(seed: int = 0, part: int = 0) -> dict:
    seeds = jax.random.split(jax.random.key(seed), 8)
    own_keys = jax.random.split(jax.random.fold_in(seeds[7], part), 8)
    queries = draw_queries(jax.random.fold_in(jax.random.fold_in(seeds[7], part), 71), part)
    keys = draw_keys(jax.random.fold_in(jax.random.fold_in(seeds[7], part), 71), part)
    values = scatter_about(own_keys[2], (TOKENS, D), 1.0, 6.0, ((0, 32),))
    text_keys = scatter_about(own_keys[3], (TXT, D), 1.7, 10.0, ((0, 32),))
    text_values = scatter_about(own_keys[4], (TXT, D), 1.0, 6.0, ((0, 32),))
    text_length = jax.random.randint(own_keys[5], (1,), TXT // 4, TXT + 1).astype(jnp.int32)
    out_weight = scatter_about(seeds[6], (D, D), D ** -0.5, 0.109375)
    return dict(queries=queries, keys=keys, values=values, text_keys=text_keys, text_values=text_values, text_length=text_length, out_weight=out_weight)


def reference(queries, keys, values, text_keys, text_values, text_length, out_weight):
    all_keys = jnp.concatenate([text_keys, keys], axis=0)
    all_values = jnp.concatenate([text_values, values], axis=0)
    usable = jnp.concatenate([jnp.arange(TXT) < text_length[0], jnp.ones((TOKENS,), dtype=bool)])
    queries_heads = queries.reshape(TOKENS, HEADS, HEAD_DIM).transpose(1, 0, 2)
    keys_heads = all_keys.reshape(TXT + TOKENS, HEADS, HEAD_DIM).transpose(1, 0, 2)
    values_heads = all_values.reshape(TXT + TOKENS, HEADS, HEAD_DIM).transpose(1, 0, 2)

    def one_head(operands):
        query_rows, key_rows, value_rows = operands
        scores = jnp.dot(query_rows, key_rows.T, preferred_element_type=jnp.float32) * (HEAD_DIM ** -0.5)
        scores = jnp.where(usable[None, :], scores, -1e30)
        highest = jnp.max(scores, axis=-1, keepdims=True)
        weights = jnp.exp(scores - highest)
        totals = jnp.sum(weights, axis=-1, keepdims=True)
        summed = jnp.dot(weights.astype(jnp.bfloat16), value_rows, preferred_element_type=jnp.float32)
        return summed / totals

    outputs = lax.map(one_head, (queries_heads, keys_heads, values_heads))
    attended = outputs.transpose(1, 0, 2).reshape(TOKENS, D).astype(jnp.bfloat16)
    return jnp.dot(attended, out_weight, preferred_element_type=jnp.float32).astype(jnp.bfloat16)
```

```python
import functools
import math

import jax
import jax.numpy as jnp
import numpy as np
from jax import lax
from jax.experimental import pallas as pl
from jax.experimental.pallas import tpu as pltpu
from jax.sharding import PartitionSpec as P

HEAD_DIM = 128
PAD = 16
MESH = pl.DeviceIdType.MESH


def kernel(
    dims,
    length_ref,
    q_ref,
    k_ref,
    v_ref,
    t_ref,
    order_ref,
    pick_ref,
    w_hbm,
    o_ref,
    qb,
    kv,
    tb,
    tkv,
    ob,
    att,
    wb,
    acc,
    local_sem,
    w_sem,
    q_send,
    kv_send,
    t_send,
    o_send,
    q_recv,
    kv_recv,
    t_recv,
    o_recv,
    kv2_send,
    kv2_recv,
    t2_send,
    t2_recv,
):
    A, R, C, X, hp = dims
    d = HEAD_DIM
    rows = q_ref.shape[0]
    seq = lax.axis_index("seq")
    core = lax.axis_index("head")
    section = lax.axis_index("section")
    a = seq // R
    r = lax.rem(seq, R)
    slot = r * C + core
    width = hp * d

    def at(a2=None, r2=None, c2=None, x2=None):
        return {
            "seq": (a if a2 is None else a2) * R + (r if r2 is None else r2),
            "head": core if c2 is None else c2,
            "section": section if x2 is None else x2,
        }

    def cols(start, size):
        return pl.ds(pl.multiple_of(start, d), size)

    def own_rows(which):
        return pl.ds(pl.multiple_of(which * rows, 16), rows)

    barrier = pltpu.get_barrier_semaphore()

    def greet(target):
        pl.semaphore_signal(barrier, inc=1, device_id=target, device_id_type=MESH)

    for da in range(A):
        for dx in range(X):
            if da or dx:
                greet(at(a2=lax.rem(a + da, A), x2=lax.rem(section + dx, X)))
    for dr in range(1, R):
        greet(at(r2=lax.rem(r + dr, R)))
    for dc in range(1, C):
        greet(at(c2=lax.rem(core + dc, C)))
    pl.semaphore_wait(barrier, A * X - 1 + R - 1 + C - 1)

    def remote(src, dst, send, recv, target):
        return pltpu.make_async_remote_copy(
            src_ref=src, dst_ref=dst, send_sem=send, recv_sem=recv, device_id=target, device_id_type=MESH
        )

    def first(j, which):
        src_cols = lambda a2: cols((a2 * hp + j) * d, d)
        if which == "kv":
            pairs = ((k_ref, 0), (v_ref, 1))
            for ref, n in pairs:
                pltpu.make_async_copy(ref.at[:, src_cols(a)], kv.at[j, n, slot, own_rows(a)], kv_recv.at[j]).start()

            def one(da, _):
                a2 = lax.rem(a + da, A)
                for ref, n in pairs:
                    remote(
                        ref.at[:, src_cols(a2)], kv.at[j, n, slot, own_rows(a)], kv_send.at[j], kv_recv.at[j], at(a2=a2)
                    ).start()
                return 0

            lax.fori_loop(1, A, one, 0)
        else:
            pltpu.make_async_copy(q_ref.at[:, src_cols(a)], qb.at[j, own_rows(a)], q_recv.at[j]).start()

            def one(da, _):
                a2 = lax.rem(a + da, A)
                remote(q_ref.at[:, src_cols(a2)], qb.at[j, own_rows(a)], q_send.at[j], q_recv.at[j], at(a2=a2)).start()
                return 0

            lax.fori_loop(1, A, one, 0)

    def first_text():
        pltpu.make_async_copy(t_ref.at[:, cols(a * width, width)], tb.at[slot, a], t_recv).start()

        def one(da, _):
            a2 = lax.rem(a + da, A)
            remote(t_ref.at[:, cols(a2 * width, width)], tb.at[slot, a], t_send, t_recv, at(a2=a2)).start()
            return 0

        lax.fori_loop(1, A, one, 0)

    first(0, "kv")
    first_text()
    first(0, "q")
    for j in range(1, hp):
        first(j, "kv")
        first(j, "q")

    weight_copies = []
    for j in range(hp):
        for b in range(X * A):
            weight_copies.append(
                pltpu.make_async_copy(
                    w_hbm.at[pl.ds((b * hp + j) * d, d)], wb.at[j, pl.ds(b * d, d)], w_sem.at[j]
                )
            )
            weight_copies[-1].start()

    def drain(ref, sem):
        pltpu.make_async_copy(ref, ref, sem).wait()

    def members():
        for dr in range(1, R):
            yield dr - 1, at(r2=lax.rem(r + dr, R))
        for dc in range(1, C):
            yield R - 2 + dc, at(c2=lax.rem(core + dc, C))

    def share(block, send, recv):
        for n, target in members():
            remote(block(slot), block(slot), send.at[n], recv.at[n], target).start()

    def forward(block, send, recv):
        base = R - 1 + C - 1
        for dr in range(1, R):
            from_slot = lax.rem(r - dr + R, R) * C + core
            drain(block(from_slot), recv.at[dr - 1])
            for dc in range(1, C):
                n = base + (dr - 1) * (C - 1) + dc - 1
                remote(
                    block(from_slot), block(from_slot), send.at[n], recv.at[n], at(c2=lax.rem(core + dc, C))
                ).start()

    def collect(block, recv):
        base = R - 1 + C - 1
        for dc in range(1, C):
            from_core = lax.rem(core - dc + C, C)
            drain(block(r * C + from_core), recv.at[R - 2 + dc])
            for dr in range(1, R):
                n = base + (dr - 1) * (C - 1) + dc - 1
                drain(block(lax.rem(r - dr + R, R) * C + from_core), recv.at[n])

    def shared_sends(block, send):
        for n in range(R - 1 + C - 1 + (R - 1) * (C - 1)):
            drain(block(slot), send.at[n])

    def kv_block(j):
        return lambda s: kv.at[j, :, s]

    def text_block(s):
        return tb.at[s]

    def share_kv(j):
        drain(kv.at[j, :, slot], kv_recv.at[j])
        share(kv_block(j), kv2_send.at[j], kv2_recv.at[j])

    def project(j):
        drain(att.at[j], o_recv.at[j])
        drain(wb.at[j], w_sem.at[j])
        columns = o_ref.shape[1]
        step = 768 if columns % 768 == 0 else d

        @pl.loop(0, columns // step)
        def _(i):
            part = pl.ds(pl.multiple_of(i * step, d), step)
            term = jnp.dot(att[j], wb[j, :, part], preferred_element_type=jnp.float32)
            if j > 0:
                term = acc[:, part] + term
            if j < hp - 1:
                acc[:, part] = term
            else:
                o_ref[:, part] = term.astype(o_ref.dtype)

    queries = qb.shape[1]
    tile = 128 if queries % 128 == 0 else rows
    scale = math.log2(math.e) * d ** (-0.5)
    nt = (((1,), (1,)), ((), ()))
    text = tkv.shape[2]

    share_kv(0)
    drain(tb.at[slot], t_recv)
    share(text_block, t2_send, t2_recv)
    for j in range(hp):
        forward(kv_block(j), kv2_send.at[j], kv2_recv.at[j])
        if j == 0:
            forward(text_block, t2_send, t2_recv)
            collect(text_block, t2_recv)
            block = tb[...].reshape(-1, width)
            for n in range(2):
                got = jnp.dot(pick_ref[n], block, preferred_element_type=jnp.float32).astype(jnp.bfloat16)
                for i in range(hp):
                    tkv[i, n] = got[:, i * d : (i + 1) * d]
        drain(qb.at[j], q_recv.at[j])
        collect(kv_block(j), kv2_recv.at[j])

        @pl.loop(0, queries // tile)
        def _(i):
            part = pl.ds(pl.multiple_of(i * tile, 16), tile)
            q = qb[j, part]
            keys = kv[j, 0].reshape(-1, d)
            values = kv[j, 1].reshape(-1, d)
            s1 = lax.dot_general(q, keys, nt, preferred_element_type=jnp.float32)
            s2 = lax.dot_general(q, tkv[j, 0], nt, preferred_element_type=jnp.float32)
            s2 = jnp.where(order_ref[...] < length_ref[0], s2, -1e30)
            top = jnp.maximum(jnp.max(s1, axis=1, keepdims=True), jnp.max(s2, axis=1, keepdims=True))
            p1 = jnp.exp2((s1 - top) * scale)
            p2 = jnp.exp2((s2 - top) * scale)
            total = jnp.sum(p1, axis=1, keepdims=True) + jnp.sum(p2, axis=1, keepdims=True)
            o = jnp.dot(p1.astype(jnp.bfloat16), values, preferred_element_type=jnp.float32)
            o = o + jnp.dot(p2.astype(jnp.bfloat16), tkv[j, 1], preferred_element_type=jnp.float32)
            ob[j, part] = (o / total).astype(jnp.bfloat16)

        column = cols((section * A + a) * d, d)
        pltpu.make_async_copy(ob.at[j, own_rows(a)], att.at[j, :, column], o_recv.at[j]).start()

        def back(da, _):
            a2 = lax.rem(a + da, A)
            for dx in range(X):
                remote(
                    ob.at[j, own_rows(a2)],
                    att.at[j, :, column],
                    o_send.at[j],
                    o_recv.at[j],
                    at(a2=a2, x2=lax.rem(section + dx, X)),
                ).start()
            return 0

        lax.fori_loop(1, A, back, 0)
        for dx in range(1, X):
            remote(
                ob.at[j, own_rows(a)],
                att.at[j, :, column],
                o_send.at[j],
                o_recv.at[j],
                at(x2=lax.rem(section + dx, X)),
            ).start()
        if j + 1 < hp:
            share_kv(j + 1)
        if j > 0:
            project(j - 1)
    project(hp - 1)

    for j in range(hp):
        if A > 1:
            drain(kv.at[j, :, slot, pl.ds(0, (A - 1) * rows)], kv_send.at[j])
            drain(qb.at[j, pl.ds(0, (A - 1) * rows)], q_send.at[j])
        if A * X > 1:
            drain(att.at[j, :, pl.ds(0, (A * X - 1) * d)], o_send.at[j])
        shared_sends(kv_block(j), kv2_send.at[j])
    if A > 1:
        drain(tb.at[slot, pl.ds(0, A - 1)], t_send)
    shared_sends(text_block, t2_send)


def shards(sizes, queries, keys, values, text_keys, text_values, text_length, out_weight):
    S, C, X = sizes
    rows, columns = queries.shape
    heads = columns // HEAD_DIM
    A = math.gcd(heads, S)
    R = S // A
    hp = heads // A
    text_rows = text_keys.shape[0]
    text = text_rows * S * C
    bf16 = jnp.bfloat16
    packed = jnp.concatenate(
        [text_keys, text_values, jnp.zeros((PAD - 2 * text_rows, columns), bf16)], axis=0
    )
    t = np.arange(text)
    block, i = t // text_rows, t % text_rows
    from_slot, from_a = block // A, block % A
    from_r, from_c = from_slot // C, from_slot % C
    order = (((from_a * R + from_r) * C + from_c) * text_rows + i).astype(np.int32)[None, :]
    pick = np.zeros((2, text, R * C * A * PAD), np.float32)
    for n in range(2):
        pick[n, t, block * PAD + n * text_rows + i] = 1.0
    pick = jnp.asarray(pick, bf16)
    out_columns = out_weight.shape[1]
    shares = R - 1 + C - 1 + (R - 1) * (C - 1)
    vmem = pl.BlockSpec(memory_space=pltpu.VMEM)
    dma = pltpu.SemaphoreType.DMA
    return pl.pallas_call(
        functools.partial(kernel, (A, R, C, X, hp)),
        out_shape=jax.ShapeDtypeStruct((rows, out_columns), bf16),
        in_specs=[pl.BlockSpec(memory_space=pltpu.SMEM)] + [vmem] * 6 + [pl.BlockSpec(memory_space=pl.ANY)],
        out_specs=vmem,
        scratch_shapes=[
            pltpu.VMEM((hp, A * rows, HEAD_DIM), bf16),
            pltpu.VMEM((hp, 2, R * C, A * rows, HEAD_DIM), bf16),
            pltpu.VMEM((R * C, A, PAD, hp * HEAD_DIM), bf16),
            pltpu.VMEM((hp, 2, text, HEAD_DIM), bf16),
            pltpu.VMEM((hp, A * rows, HEAD_DIM), bf16),
            pltpu.VMEM((hp, rows, X * A * HEAD_DIM), bf16),
            pltpu.VMEM((hp, X * A * HEAD_DIM, out_columns), bf16),
            pltpu.VMEM((rows, out_columns), jnp.float32),
            dma,
            dma((hp,)),
            dma((hp,)),
            dma((hp,)),
            dma,
            dma((hp,)),
            dma((hp,)),
            dma((hp,)),
            dma,
            dma((hp,)),
            dma((hp, shares)),
            dma((hp, shares)),
            dma((shares,)),
            dma((shares,)),
        ],
        compiler_params=pltpu.CompilerParams(
            collective_id=0, has_side_effects=True, vmem_limit_bytes=60 * 1024 * 1024
        ),
    )(text_length, queries, keys, values, packed, jnp.asarray(order), pick, out_weight)


def solution(mesh):
    sizes = (mesh.shape["seq"], mesh.shape["head"], mesh.shape["section"])
    tokens = P(("groups", "seq", "head"), "section")
    return jax.shard_map(
        functools.partial(shards, sizes),
        mesh=mesh,
        in_specs=(tokens,) * 5 + (P("groups"), P(None, "section")),
        out_specs=tokens,
        check_vma=False,
    )
```

```python
import functools
import math

import jax
import jax.numpy as jnp
import numpy as np
from jax import lax
from jax.experimental import pallas as pl
from jax.experimental.pallas import tpu as pltpu
from jax.sharding import PartitionSpec as P

HEAD_DIM = 128
MESH = pl.DeviceIdType.MESH


def kernel(
    dims,
    length_ref,
    q_ref,
    k_ref,
    v_ref,
    t_ref,
    order_ref,
    pick_hbm,
    w_hbm,
    o_ref,
    qb,
    kv,
    tb,
    tkv,
    ob,
    att,
    wb,
    acc,
    pick_ref,
    local_sem,
    w_sem,
    q_send,
    kv_send,
    t_send,
    o_send,
    q_recv,
    kv_recv,
    t_recv,
    o_recv,
    kv2_send,
    kv2_recv,
    t2_send,
    t2_recv,
):
    A, R, C, X, hp = dims
    d = HEAD_DIM
    rows = q_ref.shape[0]
    seq = lax.axis_index("seq")
    core = lax.axis_index("head")
    section = lax.axis_index("section")
    a = seq // R
    r = lax.rem(seq, R)
    slot = r * C + core
    width = hp * d

    def at(a2=None, r2=None, c2=None, x2=None):
        return {
            "seq": (a if a2 is None else a2) * R + (r if r2 is None else r2),
            "head": core if c2 is None else c2,
            "section": section if x2 is None else x2,
        }

    def cols(start, size):
        return pl.ds(pl.multiple_of(start, d), size)

    def own_rows(which):
        return pl.ds(pl.multiple_of(which * rows, 16), rows)

    barrier = pltpu.get_barrier_semaphore()

    def greet(target):
        pl.semaphore_signal(barrier, inc=1, device_id=target, device_id_type=MESH)

    for da in range(A):
        for dx in range(X):
            if da or dx:
                greet(at(a2=lax.rem(a + da, A), x2=lax.rem(section + dx, X)))
    for dr in range(1, R):
        greet(at(r2=lax.rem(r + dr, R)))
    for dc in range(1, C):
        greet(at(c2=lax.rem(core + dc, C)))
    pl.semaphore_wait(barrier, A * X - 1 + R - 1 + C - 1)

    def remote(src, dst, send, recv, target):
        return pltpu.make_async_remote_copy(
            src_ref=src, dst_ref=dst, send_sem=send, recv_sem=recv, device_id=target, device_id_type=MESH
        )

    def first(j, ref, landing, send, recv):
        src_cols = lambda a2: cols((a2 * hp + j) * d, d)
        pltpu.make_async_copy(ref.at[:, src_cols(a)], landing.at[own_rows(a)], recv).start()

        def one(da, _):
            a2 = lax.rem(a + da, A)
            remote(ref.at[:, src_cols(a2)], landing.at[own_rows(a)], send, recv, at(a2=a2)).start()
            return 0

        lax.fori_loop(1, A, one, 0)

    def first_kv(j, n):
        first(j, (k_ref, v_ref)[n], kv.at[j, n, slot], kv_send.at[j, n], kv_recv.at[j, n])

    def first_q(j):
        first(j, q_ref, qb.at[j], q_send.at[j], q_recv.at[j])

    def first_text():
        pltpu.make_async_copy(t_ref.at[:, cols(a * width, width)], tb.at[slot, a], t_recv).start()

        def one(da, _):
            a2 = lax.rem(a + da, A)
            remote(t_ref.at[:, cols(a2 * width, width)], tb.at[slot, a], t_send, t_recv, at(a2=a2)).start()
            return 0

        lax.fori_loop(1, A, one, 0)

    for j in range(hp):
        first_kv(j, 0)
        first_kv(j, 1)
        if j == 0:
            first_text()
    for j in range(hp):
        first_q(j)

    pick_copy = pltpu.make_async_copy(pick_hbm, pick_ref, local_sem)
    pick_copy.start()

    weight_copies = []
    for j in range(hp):
        for b in range(X * A):
            weight_copies.append(
                pltpu.make_async_copy(
                    w_hbm.at[pl.ds((b * hp + j) * d, d)], wb.at[j, pl.ds(b * d, d)], w_sem.at[j]
                )
            )
            weight_copies[-1].start()

    def drain(ref, sem):
        pltpu.make_async_copy(ref, ref, sem).wait()

    def members():
        for dr in range(1, R):
            yield dr - 1, at(r2=lax.rem(r + dr, R))
        for dc in range(1, C):
            yield R - 2 + dc, at(c2=lax.rem(core + dc, C))

    def share(block, send, recv):
        for n, target in members():
            remote(block(slot), block(slot), send.at[n], recv.at[n], target).start()

    def forward(block, send, recv):
        base = R - 1 + C - 1
        for dr in range(1, R):
            from_slot = lax.rem(r - dr + R, R) * C + core
            drain(block(from_slot), recv.at[dr - 1])
            for dc in range(1, C):
                n = base + (dr - 1) * (C - 1) + dc - 1
                remote(
                    block(from_slot), block(from_slot), send.at[n], recv.at[n], at(c2=lax.rem(core + dc, C))
                ).start()

    def collect(block, recv):
        base = R - 1 + C - 1
        for dc in range(1, C):
            from_core = lax.rem(core - dc + C, C)
            drain(block(r * C + from_core), recv.at[R - 2 + dc])
            for dr in range(1, R):
                n = base + (dr - 1) * (C - 1) + dc - 1
                drain(block(lax.rem(r - dr + R, R) * C + from_core), recv.at[n])

    def shared_sends(block, send):
        for n in range(R - 1 + C - 1 + (R - 1) * (C - 1)):
            drain(block(slot), send.at[n])

    def kv_block(j, n):
        return lambda s: kv.at[j, n, s]

    def text_block(s):
        return tb.at[s]

    def share_kv(j):
        for n in range(2):
            drain(kv.at[j, n, slot], kv_recv.at[j, n])
            share(kv_block(j, n), kv2_send.at[j, n], kv2_recv.at[j, n])

    def project(j):
        drain(att.at[j], o_recv.at[j])
        drain(wb.at[j], w_sem.at[j])
        columns = o_ref.shape[1]
        step = 768 if columns % 768 == 0 else d

        @pl.loop(0, columns // step)
        def _(i):
            part = pl.ds(pl.multiple_of(i * step, d), step)
            term = jnp.dot(att[j], wb[j, :, part], preferred_element_type=jnp.float32)
            if j > 0:
                term = acc[:, part] + term
            if j < hp - 1:
                acc[:, part] = term
            else:
                o_ref[:, part] = term.astype(o_ref.dtype)

    group = 2 if A % 2 == 0 else 1
    tile = group * rows
    scale = math.log2(math.e) * d ** (-0.5)
    nt = (((1,), (1,)), ((), ()))

    def attend(j, i):
        part = pl.ds(pl.multiple_of(i * tile, 16), tile)
        q = qb[j, part]
        keys = kv[j, 0].reshape(-1, d)
        values = kv[j, 1].reshape(-1, d)
        s1 = lax.dot_general(q, keys, nt, preferred_element_type=jnp.float32)
        s2 = lax.dot_general(q, tkv[j, 0], nt, preferred_element_type=jnp.float32)
        s2 = jnp.where(order_ref[...] < length_ref[0], s2, -1e30)
        top = jnp.maximum(jnp.max(s1, axis=1, keepdims=True), jnp.max(s2, axis=1, keepdims=True))
        p1 = jnp.exp2((s1 - top) * scale)
        p2 = jnp.exp2((s2 - top) * scale)
        total = jnp.sum(p1, axis=1, keepdims=True) + jnp.sum(p2, axis=1, keepdims=True)
        o = jnp.dot(p1.astype(jnp.bfloat16), values, preferred_element_type=jnp.float32)
        o = o + jnp.dot(p2.astype(jnp.bfloat16), tkv[j, 1], preferred_element_type=jnp.float32)
        ob[j, part] = (o / total).astype(jnp.bfloat16)

    column = cols((section * A + a) * d, d)

    def back(j, a2, dx):
        remote(
            ob.at[j, own_rows(a2)],
            att.at[j, :, column],
            o_send.at[j],
            o_recv.at[j],
            at(a2=a2, x2=lax.rem(section + dx, X)),
        ).start()

    def back_group(j, i):
        for b in range(group):
            for dx in range(X):
                back(j, i * group + b, dx)

    def back_own(j, i):
        for b in range(group):
            for dx in range(1, X):
                back(j, i * group + b, dx)
            if group > 1:
                @pl.when(i * group + b != a)
                def _():
                    back(j, i * group + b, 0)
        pltpu.make_async_copy(ob.at[j, own_rows(a)], att.at[j, :, column], o_recv.at[j]).start()

    own = a // group
    groups = A // group

    def attention(j):
        @pl.loop(1, groups)
        def _(di):
            i = lax.rem(own + di, groups)
            attend(j, i)
            back_group(j, i)

        attend(j, own)
        back_own(j, own)

    def forward_kv(j):
        for n in range(2):
            forward(kv_block(j, n), kv2_send.at[j, n], kv2_recv.at[j, n])

    share_kv(0)
    drain(tb.at[slot], t_recv)
    share(text_block, t2_send, t2_recv)
    for j in range(1, hp):
        share_kv(j)
        forward_kv(j - 1)
        if j == 1:
            forward(text_block, t2_send, t2_recv)
    if hp == 1:
        forward(text_block, t2_send, t2_recv)
    collect(text_block, t2_recv)
    pick_copy.wait()
    block = tb[...].reshape(-1, width)
    for n in range(2):
        got = jnp.dot(pick_ref[n], block, preferred_element_type=jnp.float32).astype(jnp.bfloat16)
        for i in range(hp):
            tkv[i, n] = got[:, i * d : (i + 1) * d]
    for j in range(hp):
        if j == hp - 1:
            forward_kv(j)
        drain(qb.at[j], q_recv.at[j])
        for n in range(2):
            collect(kv_block(j, n), kv2_recv.at[j, n])
        attention(j)
    for j in range(hp):
        project(j)

    for j in range(hp):
        for n in range(2):
            if A > 1:
                drain(kv.at[j, n, slot, pl.ds(0, (A - 1) * rows)], kv_send.at[j, n])
            shared_sends(kv_block(j, n), kv2_send.at[j, n])
        if A > 1:
            drain(qb.at[j, pl.ds(0, (A - 1) * rows)], q_send.at[j])
        if A * X > 1:
            drain(att.at[j, :, pl.ds(0, (A * X - 1) * d)], o_send.at[j])
    if A > 1:
        drain(tb.at[slot, pl.ds(0, A - 1)], t_send)
    shared_sends(text_block, t2_send)


def shards(sizes, queries, keys, values, text_keys, text_values, text_length, out_weight):
    S, C, X = sizes
    rows, columns = queries.shape
    heads = columns // HEAD_DIM
    A = math.gcd(heads, S)
    R = S // A
    hp = heads // A
    text_rows = text_keys.shape[0]
    text = text_rows * S * C
    bf16 = jnp.bfloat16
    pad = -(-2 * text_rows // 8) * 8
    packed = jnp.concatenate([text_keys, text_values], axis=0)
    packed = jnp.pad(packed, ((0, pad - 2 * text_rows), (0, 0)))
    t = np.arange(text)
    block, i = t // text_rows, t % text_rows
    from_slot, from_a = block // A, block % A
    from_r, from_c = from_slot // C, from_slot % C
    order = (((from_a * R + from_r) * C + from_c) * text_rows + i).astype(np.int32)[None, :]
    pick = np.zeros((2, text, R * C * A * pad), np.float32)
    for n in range(2):
        pick[n, t, block * pad + n * text_rows + i] = 1.0
    pick = jnp.asarray(pick, bf16)
    out_columns = out_weight.shape[1]
    shares = R - 1 + C - 1 + (R - 1) * (C - 1)
    vmem = pl.BlockSpec(memory_space=pltpu.VMEM)
    hbm = pl.BlockSpec(memory_space=pl.ANY)
    dma = pltpu.SemaphoreType.DMA
    return pl.pallas_call(
        functools.partial(kernel, (A, R, C, X, hp)),
        out_shape=jax.ShapeDtypeStruct((rows, out_columns), bf16),
        in_specs=[pl.BlockSpec(memory_space=pltpu.SMEM)] + [hbm] * 4 + [vmem] + [hbm] * 2,
        out_specs=vmem,
        scratch_shapes=[
            pltpu.VMEM((hp, A * rows, HEAD_DIM), bf16),
            pltpu.VMEM((hp, 2, R * C, A * rows, HEAD_DIM), bf16),
            pltpu.VMEM((R * C, A, pad, hp * HEAD_DIM), bf16),
            pltpu.VMEM((hp, 2, text, HEAD_DIM), bf16),
            pltpu.VMEM((hp, A * rows, HEAD_DIM), bf16),
            pltpu.VMEM((hp, rows, X * A * HEAD_DIM), bf16),
            pltpu.VMEM((hp, X * A * HEAD_DIM, out_columns), bf16),
            pltpu.VMEM((rows, out_columns), jnp.float32),
            pltpu.VMEM(pick.shape, bf16),
            dma,
            dma((hp,)),
            dma((hp,)),
            dma((hp, 2)),
            dma,
            dma((hp,)),
            dma((hp,)),
            dma((hp, 2)),
            dma,
            dma((hp,)),
            dma((hp, 2, shares)),
            dma((hp, 2, shares)),
            dma((shares,)),
            dma((shares,)),
        ],
        compiler_params=pltpu.CompilerParams(
            collective_id=0, has_side_effects=True, vmem_limit_bytes=60 * 1024 * 1024
        ),
    )(text_length, queries, keys, values, packed, jnp.asarray(order), pick, out_weight)


def solution(mesh):
    sizes = (mesh.shape["seq"], mesh.shape["head"], mesh.shape["section"])
    tokens = P(("groups", "seq", "head"), "section")
    return jax.shard_map(
        functools.partial(shards, sizes),
        mesh=mesh,
        in_specs=(tokens,) * 5 + (P("groups"), P(None, "section")),
        out_specs=tokens,
        check_vma=False,
    )
```

```python
import functools
import math

import jax
import jax.numpy as jnp
import numpy as np
from jax import lax
from jax.experimental import pallas as pl
from jax.experimental.pallas import tpu as pltpu
from jax.sharding import PartitionSpec as P

HEAD_DIM = 128
MESH = pl.DeviceIdType.MESH


def kernel(
    dims,
    length_ref,
    q_ref,
    k_ref,
    v_ref,
    tk_ref,
    tv_ref,
    order_ref,
    pick_hbm,
    w_hbm,
    o_out,
    qb,
    kv,
    tb,
    tkv,
    ob,
    att,
    wb,
    acc,
    pick_ref,
    o_ref,
    wide,
    packed,
    t_ref,
    local_sem,
    w_sem,
    q_send,
    kv_send,
    t_send,
    o_send,
    q_recv,
    kv_recv,
    t_recv,
    o_recv,
    kv2_send,
    kv2_recv,
    t2_send,
    t2_recv,
):
    A, R, C, X, hp = dims
    d = HEAD_DIM
    rows = q_ref.shape[0]
    seq = lax.axis_index("seq")
    core = lax.axis_index("head")
    section = lax.axis_index("section")
    a = seq // R
    r = lax.rem(seq, R)
    slot = r * C + core
    width = hp * d

    def at(a2=None, r2=None, c2=None, x2=None):
        return {
            "seq": (a if a2 is None else a2) * R + (r if r2 is None else r2),
            "head": core if c2 is None else c2,
            "section": section if x2 is None else x2,
        }

    def cols(start, size):
        return pl.ds(pl.multiple_of(start, d), size)

    def own_rows(which):
        return pl.ds(pl.multiple_of(which * rows, 16), rows)

    barrier = pltpu.get_barrier_semaphore()

    def greet(target):
        pl.semaphore_signal(barrier, inc=1, device_id=target, device_id_type=MESH)

    for da in range(A):
        for dx in range(X):
            if da or dx:
                greet(at(a2=lax.rem(a + da, A), x2=lax.rem(section + dx, X)))
    for dr in range(1, R):
        greet(at(r2=lax.rem(r + dr, R)))
    for dc in range(1, C):
        greet(at(c2=lax.rem(core + dc, C)))
    pl.semaphore_wait(barrier, A * X - 1 + R - 1 + C - 1)

    def remote(src, dst, send, recv, target):
        return pltpu.make_async_remote_copy(
            src_ref=src, dst_ref=dst, send_sem=send, recv_sem=recv, device_id=target, device_id_type=MESH
        )

    def first(j, ref, landing, send, recv):
        src_cols = lambda a2: cols((a2 * hp + j) * d, d)
        pltpu.make_async_copy(ref.at[:, src_cols(a)], landing.at[own_rows(a)], recv).start()

        def one(da, _):
            a2 = lax.rem(a + da, A)
            remote(ref.at[:, src_cols(a2)], landing.at[own_rows(a)], send, recv, at(a2=a2)).start()
            return 0

        lax.fori_loop(1, A, one, 0)

    def first_kv(j, n):
        first(j, (k_ref, v_ref)[n], kv.at[j, n, slot], kv_send.at[j, n], kv_recv.at[j, n])

    def first_q(j):
        first(j, q_ref, qb.at[j], q_send.at[j], q_recv.at[j])

    def first_text():
        count = tk_ref.shape[0]
        if 2 * count < wide.shape[0]:
            wide[...] = jnp.zeros_like(wide)
        wide[:count] = tk_ref[...].astype(jnp.float32)
        wide[count : 2 * count] = tv_ref[...].astype(jnp.float32)
        packed[...] = wide[...].astype(jnp.bfloat16)
        pltpu.sync_copy(packed, t_ref)
        pltpu.make_async_copy(t_ref.at[:, cols(a * width, width)], tb.at[slot, a], t_recv).start()

        def one(da, _):
            a2 = lax.rem(a + da, A)
            remote(t_ref.at[:, cols(a2 * width, width)], tb.at[slot, a], t_send, t_recv, at(a2=a2)).start()
            return 0

        lax.fori_loop(1, A, one, 0)

    for j in range(hp):
        first_kv(j, 0)
        first_kv(j, 1)
        if j == 0:
            first_text()
    for j in range(hp):
        first_q(j)

    pick_copy = pltpu.make_async_copy(pick_hbm, pick_ref, local_sem)
    pick_copy.start()

    weight_copies = []
    for j in range(hp):
        for b in range(X * A):
            weight_copies.append(
                pltpu.make_async_copy(
                    w_hbm.at[pl.ds((b * hp + j) * d, d)], wb.at[j, pl.ds(b * d, d)], w_sem.at[j]
                )
            )
            weight_copies[-1].start()

    def drain(ref, sem):
        pltpu.make_async_copy(ref, ref, sem).wait()

    def members():
        for dr in range(1, R):
            yield dr - 1, at(r2=lax.rem(r + dr, R))
        for dc in range(1, C):
            yield R - 2 + dc, at(c2=lax.rem(core + dc, C))

    def share(block, send, recv):
        for n, target in members():
            remote(block(slot), block(slot), send.at[n], recv.at[n], target).start()

    def forward(block, send, recv):
        base = R - 1 + C - 1
        for dr in range(1, R):
            from_slot = lax.rem(r - dr + R, R) * C + core
            drain(block(from_slot), recv.at[dr - 1])
            for dc in range(1, C):
                n = base + (dr - 1) * (C - 1) + dc - 1
                remote(
                    block(from_slot), block(from_slot), send.at[n], recv.at[n], at(c2=lax.rem(core + dc, C))
                ).start()

    def collect(block, recv):
        base = R - 1 + C - 1
        for dc in range(1, C):
            from_core = lax.rem(core - dc + C, C)
            drain(block(r * C + from_core), recv.at[R - 2 + dc])
            for dr in range(1, R):
                n = base + (dr - 1) * (C - 1) + dc - 1
                drain(block(lax.rem(r - dr + R, R) * C + from_core), recv.at[n])

    def shared_sends(block, send):
        for n in range(R - 1 + C - 1 + (R - 1) * (C - 1)):
            drain(block(slot), send.at[n])

    def kv_block(j, n):
        return lambda s: kv.at[j, n, s]

    def text_block(s):
        return tb.at[s]

    def share_kv(j):
        for n in range(2):
            drain(kv.at[j, n, slot], kv_recv.at[j, n])
            share(kv_block(j, n), kv2_send.at[j, n], kv2_recv.at[j, n])

    def project(j):
        drain(att.at[j], o_recv.at[j])
        drain(wb.at[j], w_sem.at[j])
        columns = o_ref.shape[1]
        step = 768 if columns % 768 == 0 else d

        @pl.loop(0, columns // step)
        def _(i):
            part = pl.ds(pl.multiple_of(i * step, d), step)
            term = jnp.dot(att[j], wb[j, :, part], preferred_element_type=jnp.float32)
            if j > 0:
                term = acc[:, part] + term
            if j < hp - 1:
                acc[:, part] = term
            else:
                o_ref[:, part] = term.astype(o_ref.dtype)

    group = 2 if A % 2 == 0 else 1
    tile = group * rows
    scale = math.log2(math.e) * d ** (-0.5)
    nt = (((1,), (1,)), ((), ()))

    def attend(j, i):
        part = pl.ds(pl.multiple_of(i * tile, 16), tile)
        q = qb[j, part]
        keys = kv[j, 0].reshape(-1, d)
        values = kv[j, 1].reshape(-1, d)
        s1 = lax.dot_general(q, keys, nt, preferred_element_type=jnp.float32)
        s2 = lax.dot_general(q, tkv[j, 0], nt, preferred_element_type=jnp.float32)
        s2 = jnp.where(order_ref[...] < length_ref[0], s2, -1e30)
        top = jnp.maximum(jnp.max(s1, axis=1, keepdims=True), jnp.max(s2, axis=1, keepdims=True))
        p1 = jnp.exp2((s1 - top) * scale)
        p2 = jnp.exp2((s2 - top) * scale)
        total = jnp.sum(p1, axis=1, keepdims=True) + jnp.sum(p2, axis=1, keepdims=True)
        o = jnp.dot(p1.astype(jnp.bfloat16), values, preferred_element_type=jnp.float32)
        o = o + jnp.dot(p2.astype(jnp.bfloat16), tkv[j, 1], preferred_element_type=jnp.float32)
        ob[j, part] = (o / total).astype(jnp.bfloat16)

    column = cols((section * A + a) * d, d)

    def back(j, a2, dx):
        remote(
            ob.at[j, own_rows(a2)],
            att.at[j, :, column],
            o_send.at[j],
            o_recv.at[j],
            at(a2=a2, x2=lax.rem(section + dx, X)),
        ).start()

    def back_group(j, i):
        for b in range(group):
            for dx in range(X):
                back(j, i * group + b, dx)

    def back_own(j, i):
        for b in range(group):
            for dx in range(1, X):
                back(j, i * group + b, dx)
            if group > 1:
                @pl.when(i * group + b != a)
                def _():
                    back(j, i * group + b, 0)
        pltpu.make_async_copy(ob.at[j, own_rows(a)], att.at[j, :, column], o_recv.at[j]).start()

    own = a // group
    groups = A // group

    def attention(j):
        @pl.loop(1, groups)
        def _(di):
            i = lax.rem(own + di, groups)
            attend(j, i)
            back_group(j, i)

        attend(j, own)
        back_own(j, own)

    def forward_kv(j):
        for n in range(2):
            forward(kv_block(j, n), kv2_send.at[j, n], kv2_recv.at[j, n])

    share_kv(0)
    drain(tb.at[slot], t_recv)
    share(text_block, t2_send, t2_recv)
    for j in range(1, hp):
        share_kv(j)
        forward_kv(j - 1)
        if j == 1:
            forward(text_block, t2_send, t2_recv)
    if hp == 1:
        forward(text_block, t2_send, t2_recv)
    collect(text_block, t2_recv)
    pick_copy.wait()
    block = tb[...].reshape(-1, width)
    for n in range(2):
        got = jnp.dot(pick_ref[n], block, preferred_element_type=jnp.float32).astype(jnp.bfloat16)
        for i in range(hp):
            tkv[i, n] = got[:, i * d : (i + 1) * d]
    for j in range(hp):
        if j == hp - 1:
            forward_kv(j)
        drain(qb.at[j], q_recv.at[j])
        for n in range(2):
            collect(kv_block(j, n), kv2_recv.at[j, n])
        attention(j)
    for j in range(hp):
        project(j)
    out_copy = pltpu.make_async_copy(o_ref, o_out, local_sem)
    out_copy.start()

    for j in range(hp):
        for n in range(2):
            if A > 1:
                drain(kv.at[j, n, slot, pl.ds(0, (A - 1) * rows)], kv_send.at[j, n])
            shared_sends(kv_block(j, n), kv2_send.at[j, n])
        if A > 1:
            drain(qb.at[j, pl.ds(0, (A - 1) * rows)], q_send.at[j])
        if A * X > 1:
            drain(att.at[j, :, pl.ds(0, (A * X - 1) * d)], o_send.at[j])
    if A > 1:
        drain(tb.at[slot, pl.ds(0, A - 1)], t_send)
    shared_sends(text_block, t2_send)
    out_copy.wait()


def shards(sizes, queries, keys, values, text_keys, text_values, text_length, out_weight):
    S, C, X = sizes
    rows, columns = queries.shape
    heads = columns // HEAD_DIM
    A = math.gcd(heads, S)
    R = S // A
    hp = heads // A
    text_rows = text_keys.shape[0]
    text = text_rows * S * C
    bf16 = jnp.bfloat16
    pad = -(-2 * text_rows // 8) * 8
    t = np.arange(text)
    block, i = t // text_rows, t % text_rows
    from_slot, from_a = block // A, block % A
    from_r, from_c = from_slot // C, from_slot % C
    order = (((from_a * R + from_r) * C + from_c) * text_rows + i).astype(np.int32)[None, :]
    pick = np.zeros((2, text, R * C * A * pad), np.float32)
    for n in range(2):
        pick[n, t, block * pad + n * text_rows + i] = 1.0
    pick = jnp.asarray(pick, bf16)
    out_columns = out_weight.shape[1]
    shares = R - 1 + C - 1 + (R - 1) * (C - 1)
    vmem = pl.BlockSpec(memory_space=pltpu.VMEM)
    hbm = pl.BlockSpec(memory_space=pl.ANY)
    dma = pltpu.SemaphoreType.DMA
    return pl.pallas_call(
        functools.partial(kernel, (A, R, C, X, hp)),
        out_shape=jax.ShapeDtypeStruct((rows, out_columns), bf16),
        in_specs=[pl.BlockSpec(memory_space=pltpu.SMEM)] + [hbm] * 3 + [vmem] * 3 + [hbm] * 2,
        out_specs=pl.BlockSpec(memory_space=pl.ANY),
        scratch_shapes=[
            pltpu.VMEM((hp, A * rows, HEAD_DIM), bf16),
            pltpu.VMEM((hp, 2, R * C, A * rows, HEAD_DIM), bf16),
            pltpu.VMEM((R * C, A, pad, hp * HEAD_DIM), bf16),
            pltpu.VMEM((hp, 2, text, HEAD_DIM), bf16),
            pltpu.VMEM((hp, A * rows, HEAD_DIM), bf16),
            pltpu.VMEM((hp, rows, X * A * HEAD_DIM), bf16),
            pltpu.VMEM((hp, X * A * HEAD_DIM, out_columns), bf16),
            pltpu.VMEM((rows, out_columns), jnp.float32),
            pltpu.VMEM(pick.shape, bf16),
            pltpu.VMEM((rows, out_columns), bf16),
            pltpu.VMEM((pad, columns), jnp.float32),
            pltpu.VMEM((pad, columns), bf16),
            pltpu.VMEM((pad, columns), bf16),
            dma,
            dma((hp,)),
            dma((hp,)),
            dma((hp, 2)),
            dma,
            dma((hp,)),
            dma((hp,)),
            dma((hp, 2)),
            dma,
            dma((hp,)),
            dma((hp, 2, shares)),
            dma((hp, 2, shares)),
            dma((shares,)),
            dma((shares,)),
        ],
        compiler_params=pltpu.CompilerParams(
            collective_id=0, has_side_effects=True, vmem_limit_bytes=60 * 1024 * 1024
        ),
    )(text_length, queries, keys, values, text_keys, text_values, jnp.asarray(order), pick, out_weight)


def solution(mesh):
    sizes = (mesh.shape["seq"], mesh.shape["head"], mesh.shape["section"])
    tokens = P(("groups", "seq", "head"), "section")
    return jax.shard_map(
        functools.partial(shards, sizes),
        mesh=mesh,
        in_specs=(tokens,) * 5 + (P("groups"), P(None, "section")),
        out_specs=tokens,
        check_vma=False,
    )
```

```python
import functools
import math

import jax
import jax.numpy as jnp
import numpy as np
from jax import lax
from jax.experimental import pallas as pl
from jax.experimental.pallas import tpu as pltpu
from jax.sharding import PartitionSpec as P

HEAD_DIM = 128
MESH = pl.DeviceIdType.MESH


def kernel(
    dims,
    length_ref,
    q_ref,
    k_ref,
    v_ref,
    tk_ref,
    tv_ref,
    order_ref,
    pick_hbm,
    w_hbm,
    o_out,
    qb,
    kv,
    tb,
    tkv,
    ob,
    att,
    wb,
    acc,
    pick_ref,
    o_ref,
    wide,
    packed,
    t_ref,
    local_sem,
    w_sem,
    q_send,
    kv_send,
    t_send,
    o_send,
    q_recv,
    kv_recv,
    t_recv,
    o_recv,
    kv2_send,
    kv2_recv,
    t2_send,
    t2_recv,
):
    A, R, C, X, hp = dims
    d = HEAD_DIM
    rows = q_ref.shape[0]
    seq = lax.axis_index("seq")
    core = lax.axis_index("head")
    section = lax.axis_index("section")
    a = seq // R
    r = lax.rem(seq, R)
    slot = r * C + core
    width = hp * d

    def at(a2=None, r2=None, c2=None, x2=None):
        return {
            "seq": (a if a2 is None else a2) * R + (r if r2 is None else r2),
            "head": core if c2 is None else c2,
            "section": section if x2 is None else x2,
        }

    def cols(start, size):
        return pl.ds(pl.multiple_of(start, d), size)

    def own_rows(which):
        return pl.ds(pl.multiple_of(which * rows, 16), rows)

    barrier = pltpu.get_barrier_semaphore()

    def greet(target):
        pl.semaphore_signal(barrier, inc=1, device_id=target, device_id_type=MESH)

    for da in range(A):
        for dx in range(X):
            if da or dx:
                greet(at(a2=lax.rem(a + da, A), x2=lax.rem(section + dx, X)))
    for dr in range(1, R):
        greet(at(r2=lax.rem(r + dr, R)))
    for dc in range(1, C):
        greet(at(c2=lax.rem(core + dc, C)))
    pl.semaphore_wait(barrier, A * X - 1 + R - 1 + C - 1)

    def remote(src, dst, send, recv, target):
        return pltpu.make_async_remote_copy(
            src_ref=src, dst_ref=dst, send_sem=send, recv_sem=recv, device_id=target, device_id_type=MESH
        )

    def first(j, ref, landing, send, recv):
        src_cols = lambda a2: cols((a2 * hp + j) * d, d)
        pltpu.make_async_copy(ref.at[:, src_cols(a)], landing.at[own_rows(a)], recv).start()

        def one(da, _):
            a2 = lax.rem(a + da, A)
            remote(ref.at[:, src_cols(a2)], landing.at[own_rows(a)], send, recv, at(a2=a2)).start()
            return 0

        lax.fori_loop(1, A, one, 0)

    def first_kv(j, n):
        first(j, (k_ref, v_ref)[n], kv.at[j, n, slot], kv_send.at[j, n], kv_recv.at[j, n])

    def first_q(j):
        first(j, q_ref, qb.at[j], q_send.at[j], q_recv.at[j])

    def first_text():
        count = tk_ref.shape[0]
        if 2 * count < wide.shape[0]:
            wide[...] = jnp.zeros_like(wide)
        wide[:count] = tk_ref[...].astype(jnp.float32)
        wide[count : 2 * count] = tv_ref[...].astype(jnp.float32)
        packed[...] = wide[...].astype(jnp.bfloat16)
        pltpu.sync_copy(packed, t_ref)
        pltpu.make_async_copy(t_ref.at[:, cols(a * width, width)], tb.at[slot, a], t_recv).start()

        def one(da, _):
            a2 = lax.rem(a + da, A)
            remote(t_ref.at[:, cols(a2 * width, width)], tb.at[slot, a], t_send, t_recv, at(a2=a2)).start()
            return 0

        lax.fori_loop(1, A, one, 0)

    for j in range(hp):
        first_kv(j, 0)
        first_kv(j, 1)
        if j == 0:
            first_text()
    for j in range(hp):
        first_q(j)

    pick_copy = pltpu.make_async_copy(pick_hbm, pick_ref, local_sem)
    pick_copy.start()

    weight_copies = []
    for j in range(hp):
        for b in range(X * A):
            weight_copies.append(
                pltpu.make_async_copy(
                    w_hbm.at[pl.ds((b * hp + j) * d, d)], wb.at[j, pl.ds(b * d, d)], w_sem.at[j]
                )
            )
            weight_copies[-1].start()

    def drain(ref, sem):
        pltpu.make_async_copy(ref, ref, sem).wait()

    def members():
        for dr in range(1, R):
            yield dr - 1, at(r2=lax.rem(r + dr, R))
        for dc in range(1, C):
            yield R - 2 + dc, at(c2=lax.rem(core + dc, C))

    def share(block, send, recv):
        for n, target in members():
            remote(block(slot), block(slot), send.at[n], recv.at[n], target).start()

    def forward(block, send, recv):
        base = R - 1 + C - 1
        for dr in range(1, R):
            from_slot = lax.rem(r - dr + R, R) * C + core
            drain(block(from_slot), recv.at[dr - 1])
            for dc in range(1, C):
                n = base + (dr - 1) * (C - 1) + dc - 1
                remote(
                    block(from_slot), block(from_slot), send.at[n], recv.at[n], at(c2=lax.rem(core + dc, C))
                ).start()

    def collect(block, recv):
        base = R - 1 + C - 1
        for dc in range(1, C):
            from_core = lax.rem(core - dc + C, C)
            drain(block(r * C + from_core), recv.at[R - 2 + dc])
            for dr in range(1, R):
                n = base + (dr - 1) * (C - 1) + dc - 1
                drain(block(lax.rem(r - dr + R, R) * C + from_core), recv.at[n])

    def shared_sends(block, send):
        for n in range(R - 1 + C - 1 + (R - 1) * (C - 1)):
            drain(block(slot), send.at[n])

    def kv_block(j, n):
        return lambda s: kv.at[j, n, s]

    def text_block(s):
        return tb.at[s]

    def share_kv(j):
        for n in range(2):
            drain(kv.at[j, n, slot], kv_recv.at[j, n])
            share(kv_block(j, n), kv2_send.at[j, n], kv2_recv.at[j, n])

    def project(j):
        drain(att.at[j], o_recv.at[j])
        drain(wb.at[j], w_sem.at[j])
        columns = o_ref.shape[1]
        step = 768 if columns % 768 == 0 else d

        @pl.loop(0, columns // step)
        def _(i):
            part = pl.ds(pl.multiple_of(i * step, d), step)
            term = jnp.dot(att[j], wb[j, :, part], preferred_element_type=jnp.float32)
            if j > 0:
                term = acc[:, part] + term
            if j < hp - 1:
                acc[:, part] = term
            else:
                o_ref[:, part] = term.astype(o_ref.dtype)

    group = 1
    tile = group * rows
    scale = math.log2(math.e) * d ** (-0.5)
    nt = (((1,), (1,)), ((), ()))

    def attend(j, i):
        part = pl.ds(pl.multiple_of(i * tile, 16), tile)
        q = qb[j, part]
        keys = kv[j, 0].reshape(-1, d)
        values = kv[j, 1].reshape(-1, d)
        s1 = lax.dot_general(q, keys, nt, preferred_element_type=jnp.float32)
        s2 = lax.dot_general(q, tkv[j, 0], nt, preferred_element_type=jnp.float32)
        s2 = jnp.where(order_ref[...] < length_ref[0], s2, -1e30)
        top = jnp.maximum(jnp.max(s1, axis=1, keepdims=True), jnp.max(s2, axis=1, keepdims=True))
        p1 = jnp.exp2((s1 - top) * scale)
        p2 = jnp.exp2((s2 - top) * scale)
        total = jnp.sum(p1, axis=1, keepdims=True) + jnp.sum(p2, axis=1, keepdims=True)
        o = jnp.dot(p1.astype(jnp.bfloat16), values, preferred_element_type=jnp.float32)
        o = o + jnp.dot(p2.astype(jnp.bfloat16), tkv[j, 1], preferred_element_type=jnp.float32)
        ob[j, part] = (o / total).astype(jnp.bfloat16)

    column = cols((section * A + a) * d, d)

    def back(j, a2, dx):
        remote(
            ob.at[j, own_rows(a2)],
            att.at[j, :, column],
            o_send.at[j],
            o_recv.at[j],
            at(a2=a2, x2=lax.rem(section + dx, X)),
        ).start()

    def back_group(j, i):
        for b in range(group):
            for dx in range(X):
                back(j, i * group + b, dx)

    def back_own(j, i):
        for b in range(group):
            for dx in range(1, X):
                back(j, i * group + b, dx)
            if group > 1:
                @pl.when(i * group + b != a)
                def _():
                    back(j, i * group + b, 0)
        pltpu.make_async_copy(ob.at[j, own_rows(a)], att.at[j, :, column], o_recv.at[j]).start()

    own = a // group
    groups = A // group

    def attention(j):
        @pl.loop(1, groups)
        def _(di):
            i = lax.rem(own + di, groups)
            attend(j, i)
            back_group(j, i)

        attend(j, own)
        back_own(j, own)

    def forward_kv(j):
        for n in range(2):
            forward(kv_block(j, n), kv2_send.at[j, n], kv2_recv.at[j, n])

    share_kv(0)
    drain(tb.at[slot], t_recv)
    share(text_block, t2_send, t2_recv)
    for j in range(1, hp):
        share_kv(j)
        forward_kv(j - 1)
        if j == 1:
            forward(text_block, t2_send, t2_recv)
    if hp == 1:
        forward(text_block, t2_send, t2_recv)
    collect(text_block, t2_recv)
    pick_copy.wait()
    block = tb[...].reshape(-1, width)
    for n in range(2):
        got = jnp.dot(pick_ref[n], block, preferred_element_type=jnp.float32).astype(jnp.bfloat16)
        for i in range(hp):
            tkv[i, n] = got[:, i * d : (i + 1) * d]
    for j in range(hp):
        if j == hp - 1:
            forward_kv(j)
        drain(qb.at[j], q_recv.at[j])
        for n in range(2):
            collect(kv_block(j, n), kv2_recv.at[j, n])
        attention(j)
    for j in range(hp):
        project(j)
    out_copy = pltpu.make_async_copy(o_ref, o_out, local_sem)
    out_copy.start()

    for j in range(hp):
        for n in range(2):
            if A > 1:
                drain(kv.at[j, n, slot, pl.ds(0, (A - 1) * rows)], kv_send.at[j, n])
            shared_sends(kv_block(j, n), kv2_send.at[j, n])
        if A > 1:
            drain(qb.at[j, pl.ds(0, (A - 1) * rows)], q_send.at[j])
        if A * X > 1:
            drain(att.at[j, :, pl.ds(0, (A * X - 1) * d)], o_send.at[j])
    if A > 1:
        drain(tb.at[slot, pl.ds(0, A - 1)], t_send)
    shared_sends(text_block, t2_send)
    out_copy.wait()


def shards(sizes, queries, keys, values, text_keys, text_values, text_length, out_weight):
    S, C, X = sizes
    rows, columns = queries.shape
    heads = columns // HEAD_DIM
    A = math.gcd(heads, S)
    R = S // A
    hp = heads // A
    text_rows = text_keys.shape[0]
    text = text_rows * S * C
    bf16 = jnp.bfloat16
    pad = -(-2 * text_rows // 8) * 8
    t = np.arange(text)
    block, i = t // text_rows, t % text_rows
    from_slot, from_a = block // A, block % A
    from_r, from_c = from_slot // C, from_slot % C
    order = (((from_a * R + from_r) * C + from_c) * text_rows + i).astype(np.int32)[None, :]
    pick = np.zeros((2, text, R * C * A * pad), np.float32)
    for n in range(2):
        pick[n, t, block * pad + n * text_rows + i] = 1.0
    pick = jnp.asarray(pick, bf16)
    out_columns = out_weight.shape[1]
    shares = R - 1 + C - 1 + (R - 1) * (C - 1)
    vmem = pl.BlockSpec(memory_space=pltpu.VMEM)
    hbm = pl.BlockSpec(memory_space=pl.ANY)
    dma = pltpu.SemaphoreType.DMA
    return pl.pallas_call(
        functools.partial(kernel, (A, R, C, X, hp)),
        out_shape=jax.ShapeDtypeStruct((rows, out_columns), bf16),
        in_specs=[pl.BlockSpec(memory_space=pltpu.SMEM)] + [hbm] * 3 + [vmem] * 3 + [hbm] * 2,
        out_specs=pl.BlockSpec(memory_space=pl.ANY),
        scratch_shapes=[
            pltpu.VMEM((hp, A * rows, HEAD_DIM), bf16),
            pltpu.VMEM((hp, 2, R * C, A * rows, HEAD_DIM), bf16),
            pltpu.VMEM((R * C, A, pad, hp * HEAD_DIM), bf16),
            pltpu.VMEM((hp, 2, text, HEAD_DIM), bf16),
            pltpu.VMEM((hp, A * rows, HEAD_DIM), bf16),
            pltpu.VMEM((hp, rows, X * A * HEAD_DIM), bf16),
            pltpu.VMEM((hp, X * A * HEAD_DIM, out_columns), bf16),
            pltpu.VMEM((rows, out_columns), jnp.float32),
            pltpu.VMEM(pick.shape, bf16),
            pltpu.VMEM((rows, out_columns), bf16),
            pltpu.VMEM((pad, columns), jnp.float32),
            pltpu.VMEM((pad, columns), bf16),
            pltpu.VMEM((pad, columns), bf16),
            dma,
            dma((hp,)),
            dma((hp,)),
            dma((hp, 2)),
            dma,
            dma((hp,)),
            dma((hp,)),
            dma((hp, 2)),
            dma,
            dma((hp,)),
            dma((hp, 2, shares)),
            dma((hp, 2, shares)),
            dma((shares,)),
            dma((shares,)),
        ],
        compiler_params=pltpu.CompilerParams(
            collective_id=0, has_side_effects=True, vmem_limit_bytes=60 * 1024 * 1024
        ),
    )(text_length, queries, keys, values, text_keys, text_values, jnp.asarray(order), pick, out_weight)


def solution(mesh):
    sizes = (mesh.shape["seq"], mesh.shape["head"], mesh.shape["section"])
    tokens = P(("groups", "seq", "head"), "section")
    return jax.shard_map(
        functools.partial(shards, sizes),
        mesh=mesh,
        in_specs=(tokens,) * 5 + (P("groups"), P(None, "section")),
        out_specs=tokens,
        check_vma=False,
    )
```
